32 devices in a mesh: rock: 4 (over y, x), frac: 8 (over z, core).
Axes of the slice: x: 2, y: 2, z: 4, core: 2. Of those that a mesh axis runs over, the one named last changes fastest.
Arguments:
- jumps: float32 [3, 32768, 128], P(None, ('rock', 'frac')), may hold values from -6 to 6
- base_aperture: float32 [32768, 128], P(('rock', 'frac')), may hold values from 1 to 3
- pressure: float32 [16, 32768, 128], P(None, ('rock', 'frac')), may hold values from -6 to 6
- block_fracture: int32 [32768], P(('rock', 'frac')), may hold values from 0 to 4095, never falling along the last dimension, each value on 1 to 32 neighbouring positions
- send_face: int32 [65536], P(('rock', 'frac')), may hold values from 0 to 1024, as said below
- elem_source: int32 [32768], P(('rock', 'frac')), may hold values from 0 to 2047, as said below
- pair_local: int32 [2048], P(('rock', 'frac')), may hold values from 0 to 1024, as said below
- send_block: int32 [2048], P(('rock', 'frac')), may hold values from 0 to 1024, as said below
- tiles: bfloat16 [2048, 128, 128], P(('rock', 'frac')), may hold values from 0 to 0.015625
Outputs:
- image: float32 [16, 32768, 128], P(None, ('rock', 'frac'))
- aperture: float32 [32768, 128], P(('rock', 'frac'))
The draws below stay inside these ranges and needn't reach their ends.
Inputs may be any that keep to these rules, and one draw needn't show every extreme that they name: `send_face`: entry r * 512 + m of a device's block names the local face block that it sends as the m-th to the device of rock index r in its frac column, or 1024 for an empty slot; each face block is sent once; every device fills all 512 slots to one destination and receives 512 from one source. `elem_source`: the entry s * 512 + m of an element block names slot m of what the device of rock index s in the same frac column sends to its device; every filled slot is named once and no empty one. `pair_local`: entry q * 8 + c of a device's block is the local element block of its c-th intersection with the device of frac index q in its rock row, or 1024 for an empty slot; each device fills all 8 slots to at least one peer. `send_block`: entry q * 8 + c of a device's block is its local element block in the c-th intersection stored by the device of frac index q in the same rock row; it is 1024 exactly when that slot there is empty.
All inputs are finite; a program needn't handle non-finite values.
Results may differ from the reference program's by a relative error of at most 0.0003.
Values sent between devices are 32-bit elements; how exact they have to be, the bound alone decides.
A program may use at most 128 MiB of HBM per device.

```python
import math
import jax
import jax.numpy as jnp
import numpy as np
from jax import lax

BLOCK = 128
EB_DEV = 1024
NV = 16
CAP = 8
CAPF = 512
EBLK = 32768
FRACS = 4096
N_ROCK = 4
N_FRAC = 8
DEVICES = 32


def shuffled(subkey):
    return jax.random.permutation(subkey, EB_DEV).astype(jnp.int32)


def face_plan(key):
    base_key = jax.random.fold_in(key, 11)
    turn_key, source_key, target_key = jax.random.split(base_key, 3)
    rotation = jax.random.randint(turn_key, (N_FRAC,), 0, N_ROCK)
    shares = jnp.array([EB_DEV // 2, EB_DEV // 4, EB_DEV // 8, EB_DEV // 8], jnp.int32)
    rocks = jnp.arange(N_ROCK, dtype=jnp.int32)
    offset = (rocks[None, None, :] - rocks[None, :, None] + rotation[:, None, None]) % N_ROCK
    counts = shares[offset]
    send_end = jnp.cumsum(counts, axis=2)
    send_start = send_end - counts
    recv_end = jnp.swapaxes(jnp.cumsum(counts, axis=1), 1, 2)
    recv_start = recv_end - jnp.swapaxes(counts, 1, 2)
    order = jnp.arange(EB_DEV, dtype=jnp.int32)
    source_perm = jax.vmap(shuffled)(jax.random.split(source_key, N_FRAC * N_ROCK)).reshape(N_FRAC, N_ROCK, EB_DEV)
    target_perm = jax.vmap(shuffled)(jax.random.split(target_key, N_FRAC * N_ROCK)).reshape(N_FRAC, N_ROCK, EB_DEV)
    target_rock = jnp.sum((order[None, None, :, None] >= send_end[:, :, None, :]).astype(jnp.int32), axis=3)
    position = order[None, None, :] - jnp.take_along_axis(send_start, target_rock, axis=2)
    column_grid = jnp.arange(N_FRAC, dtype=jnp.int32)[:, None, None]
    rock_grid = rocks[None, :, None]
    table = jnp.full((N_FRAC, N_ROCK, N_ROCK * CAPF), EB_DEV, jnp.int32)
    table = table.at[column_grid, rock_grid, target_rock * CAPF + position].set(source_perm)
    source_rock = jnp.sum((order[None, None, :, None] >= recv_end[:, :, None, :]).astype(jnp.int32), axis=3)
    arrival = order[None, None, :] - jnp.take_along_axis(recv_start, source_rock, axis=2)
    plan = jnp.zeros((N_FRAC, N_ROCK, EB_DEV), jnp.int32)
    plan = plan.at[column_grid, rock_grid, target_perm].set(source_rock * CAPF + arrival)
    return (jnp.swapaxes(table, 0, 1).reshape(-1), jnp.swapaxes(plan, 0, 1).reshape(-1))


def pair_plan(key):
    base_key = jax.random.fold_in(key, 23)
    keys = jax.random.split(base_key, 5)
    shape = (N_ROCK, N_FRAC, N_FRAC, CAP)
    rate = jax.random.randint(keys[0], (N_ROCK, N_FRAC, 1, 1), 1, 5)
    rotation = jax.random.randint(keys[1], (N_ROCK, N_FRAC, 1), 0, N_FRAC)
    coin = jax.random.randint(keys[2], shape, 0, 4)
    peers = jnp.arange(N_FRAC, dtype=jnp.int32)
    favoured = peers[None, None, :] == (peers[None, :, None] + rotation) % N_FRAC
    valid = (coin < rate) | favoured[..., None]
    holder = jax.random.randint(keys[3], shape, 0, EB_DEV)
    partner = jax.random.randint(keys[4], shape, 0, EB_DEV)
    stored = jnp.where(valid, holder, EB_DEV).astype(jnp.int32).reshape(-1)
    served = jnp.swapaxes(jnp.where(valid, partner, EB_DEV), 1, 2).astype(jnp.int32).reshape(-1)
    return (stored, served)


def draw_send_face(key, part):
    return face_plan(key)[0]


def draw_elem_source(key, part):
    return face_plan(key)[1]


def draw_pair_local(key, part):
    return pair_plan(key)[0]


def draw_send_block(key, part):
    return pair_plan(key)[1]


def steps_of(key, extent, shards, low, top_value):
    gain = 1.0
    for dim, blocks in shards:
        draws = jax.random.uniform(jax.random.fold_in(jax.random.fold_in(key, 6), dim), (blocks,), jnp.float32, low / len(shards), top_value / len(shards))
        gain = gain * jnp.repeat(jnp.exp(draws), extent[dim] // blocks).reshape((-1,) + (1,) * (len(extent) - 1 - dim))
    return gain


def length_profile(amount, total, limit, lean):
    weights = [(1 << 20) // math.isqrt(rank ** lean) + 1 for rank in range(2, amount + 1)]
    spare, holding = total - limit - (amount - 1), [1] * (amount - 1)
    while spare > 0:
        candidates = [i for i in range(amount - 1) if holding[i] < limit]
        whole, remaining = sum([weights[i] for i in candidates]), spare
        for i in candidates:
            addition = min(limit - holding[i], max(1, remaining * weights[i] // whole), spare)
            holding[i] = holding[i] + addition
            spare = spare - addition
    return np.array([limit] + holding)


def uneven_parts(stream_key, count, total, most, skew):
    if count == 2:
        one = jax.random.randint(stream_key, (), max(1, total - most), min(most, total - 1) + 1)
        return jnp.stack([one, total - one])
    lengths = jnp.asarray(length_profile(count, total, most, skew), jnp.int32)
    pairs = (count - 1) // 2
    source_of, receiver = lengths[1:1 + 2 * pairs:2], lengths[2:2 + 2 * pairs:2]
    margin = jnp.minimum(source_of - 1, most - receiver)
    passed = jax.random.randint(jax.random.fold_in(stream_key, 1), (pairs,), 0, 1 << 20) % (margin + 1)
    lengths = lengths.at[1:1 + 2 * pairs:2].set(source_of - passed).at[2:2 + 2 * pairs:2].set(receiver + passed)
    return lengths[jax.random.permutation(jax.random.fold_in(stream_key, 2), count)]


def centred(rng, extent, spread, limit, shards=(), kind=jnp.bfloat16):
    values = jax.random.normal(rng, extent, jnp.float32) * spread
    if len(shards) > 0:
        values = steps_of(rng, extent, shards, -0.22, 0.18) * values
    return jnp.clip(values, min=-limit, max=limit).astype(kind)


def setup_inputs(seed: int = 0) -> dict:
    key_list = jax.random.split(jax.random.key(seed), 10)
    return {
        "jumps": centred(key_list[0], (3, EBLK, BLOCK), 1.0, 6.0, ((1, 32),), jnp.float32),
        "base_aperture": jnp.clip(jnp.exp(math.log(3.0) - 1.0986123 * jax.random.uniform(key_list[1], (EBLK, BLOCK), jnp.float32) ** steps_of(key_list[1], (EBLK, BLOCK), ((0, 32),), -0.2, 0.2)), 1.0, 3.0),
        "pressure": centred(key_list[2], (NV, EBLK, BLOCK), 1.0, 6.0, ((1, 32),), jnp.float32),
        "block_fracture": jnp.searchsorted(jnp.cumsum(uneven_parts(key_list[3], FRACS, EBLK, 32, 0)), jnp.arange(EBLK), side="right").astype(jnp.int32),
        "send_face": draw_send_face(jax.random.fold_in(key_list[9], 71), 0),
        "elem_source": draw_elem_source(jax.random.fold_in(key_list[9], 71), 0),
        "pair_local": draw_pair_local(jax.random.fold_in(key_list[9], 71), 0),
        "send_block": draw_send_block(jax.random.fold_in(key_list[9], 71), 0),
        "tiles": jnp.clip(0.015625 * jax.random.uniform(key_list[8], (DEVICES * N_FRAC * CAP, BLOCK, BLOCK), jnp.float32) ** steps_of(key_list[8], (DEVICES * N_FRAC * CAP, BLOCK, BLOCK), ((0, 32),), -0.2, 0.2), 0.0, 0.015625).astype(jnp.bfloat16),
    }


def reference(jumps, base_aperture, pressure, block_fracture, send_face, elem_source, pair_local, send_block, tiles):
    device_of = jnp.arange(EBLK, dtype=jnp.int32) // EB_DEV
    rock_index = device_of // N_FRAC
    column = device_of % N_FRAC
    source_rock = elem_source // CAPF
    slot_index = elem_source % CAPF
    sender = source_rock * N_FRAC + column
    local_face = send_face[sender * (N_ROCK * CAPF) + rock_index * CAPF + slot_index]
    face_index = (sender * EB_DEV + local_face).astype(jnp.int32)
    picked = jumps[:, face_index, :]
    aperture = base_aperture + 0.5 * jax.nn.softplus(picked[0]) + 0.2 * (jnp.sqrt(1.0 + picked[1] ** 2 + picked[2] ** 2) - 1.0)
    trans = aperture ** 3 / 12.0
    image = aperture[None] * pressure
    flat_press = pressure.reshape(NV, -1)
    flat_trans = trans.reshape(-1)
    fracture = jnp.repeat(block_fracture, BLOCK)
    joined = (fracture[:-1] == fracture[1:]).astype(jnp.float32)
    left_trans = flat_trans[:-1]
    right_trans = flat_trans[1:]
    half_trans = 2.0 * left_trans * right_trans / (left_trans + right_trans) * joined
    flux = half_trans[None] * (flat_press[:, :-1] - flat_press[:, 1:])
    chain = jnp.pad(flux, ((0, 0), (0, 1))) - jnp.pad(flux, ((0, 0), (1, 0)))
    image = image + chain.reshape(NV, EBLK, BLOCK)
    layout = (N_ROCK, N_FRAC, N_FRAC, CAP)
    holder = pair_local.reshape(layout)
    partner = jnp.swapaxes(send_block.reshape(layout), 1, 2)
    rock_rows = jnp.arange(N_ROCK, dtype=jnp.int32)[:, None, None, None]
    owner = rock_rows * N_FRAC + jnp.arange(N_FRAC, dtype=jnp.int32)[None, :, None, None]
    peer = rock_rows * N_FRAC + jnp.arange(N_FRAC, dtype=jnp.int32)[None, None, :, None]
    live = holder < EB_DEV
    near_rows = jnp.where(live, owner * EB_DEV + holder, EBLK).astype(jnp.int32).reshape(DEVICES, -1)
    far_rows = jnp.where(live, peer * EB_DEV + partner, EBLK).astype(jnp.int32).reshape(DEVICES, -1)
    trans_padded = jnp.concatenate([trans, jnp.ones((1, BLOCK), jnp.float32)], axis=0)
    press_padded = jnp.concatenate([pressure, jnp.zeros((NV, 1, BLOCK), jnp.float32)], axis=1)
    low_padded = lax.optimization_barrier(press_padded.astype(jnp.bfloat16)).astype(jnp.float32)
    tile_groups = tiles.reshape(DEVICES, N_FRAC * CAP, BLOCK, BLOCK)

    def visit(total, items):
        tile_group, near_index, far_index = items
        near_trans = trans_padded[near_index]
        far_trans = trans_padded[far_index]
        near_press = press_padded[:, near_index]
        far_press = press_padded[:, far_index]
        near_low = low_padded[:, near_index]
        far_low = low_padded[:, far_index]
        mask = (near_index < EBLK).astype(jnp.float32)
        weights = tile_group.astype(jnp.float32) * (2.0 * near_trans[:, :, None] * far_trans[:, None, :] / (near_trans[:, :, None] + far_trans[:, None, :])) * mask[:, None, None]
        low_weights = lax.optimization_barrier(weights.astype(jnp.bfloat16)).astype(jnp.float32)
        near_term = lax.optimization_barrier(jnp.sum(weights, axis=2))[None] * near_press - jnp.einsum('sab,vsb->vsa', low_weights, far_low, precision=lax.Precision.HIGHEST)
        far_term = lax.optimization_barrier(jnp.sum(weights, axis=1))[None] * far_press - jnp.einsum('sab,vsa->vsb', low_weights, near_low, precision=lax.Precision.HIGHEST)
        total = total.at[:, near_index].add(near_term)
        total = total.at[:, far_index].add(far_term)
        return (total, None)
    start = jnp.zeros((NV, EBLK + 1, BLOCK), jnp.float32)
    cross, unused = lax.scan(visit, start, (tile_groups, near_rows, far_rows))
    image = image + cross[:, :EBLK]
    return (image, aperture)
```

```python
import functools

import jax
import jax.numpy as jnp
from jax import lax
from jax.experimental import pallas as pl
from jax.experimental.pallas import tpu as pltpu
from jax.sharding import PartitionSpec as P

MESH = pl.DeviceIdType.MESH
F32 = jnp.float32
BF16 = jnp.bfloat16
LANES = 128
VMEM_LIMIT = 60 * 1024 * 1024


def split(x):
    hi = x.astype(BF16)
    return hi, (x - hi.astype(F32)).astype(BF16)


def split_lanes(x):
    return jnp.concatenate(split(x), axis=1)


def fold(x):
    half = x.shape[1] // 2
    return x[:, :half] + x[:, half:]


def column(row):
    return jnp.broadcast_to(row, (LANES, LANES)).T


def one_hot(col, width):
    lane = lax.broadcasted_iota(jnp.int32, (LANES, LANES), 1)
    parts = [
        jnp.where(col == lane + k * LANES, 1.0, 0.0).astype(BF16) for k in range(width // LANES)
    ]
    return jnp.concatenate(parts, axis=1)


def dot(a, b):
    return jnp.dot(a, b, preferred_element_type=F32)


def dot_nt(a, b):
    return lax.dot_general(a, b, (((1,), (1,)), ((), ())), preferred_element_type=F32)


def exchange_kernel(
    nr,
    nf,
    jumps_hbm,
    base_hbm,
    press_hbm,
    tiles_hbm,
    face_ref,
    elem_ref,
    slot_ref,
    frac_ref,
    ap_ref,
    terms_ref,
    left_ref,
    right_ref,
    jumps,
    base,
    press,
    tiles,
    gap,
    face_out,
    face_in,
    elem_hot,
    pair_hot,
    acc,
    near_p,
    far_out,
    far_in,
    near_t,
    trans_out,
    trans_in,
    near_term,
    ret_out,
    ret_in,
    edge_out,
    load_sem,
    face_ss,
    face_rs,
    far_ss,
    far_rs,
    trans_ss,
    trans_rs,
    ret_ss,
    ret_rs,
    edge_ss,
    edge_rs,
):
    me_r = lax.axis_index("rock")
    me_f = lax.axis_index("frac")
    nv, eb, width = press.shape
    cap = far_in.shape[2]
    slots = nf * cap
    capf = face_in.shape[1]
    nsub = capf // LANES
    count = nr * nf
    me = me_r * nf + me_f
    after = lax.rem(me + 1, count)
    before = lax.rem(me + count - 1, count)
    after_id = (after // nf, lax.rem(after, nf))
    before_id = (before // nf, lax.rem(before, nf))

    loads = [
        pltpu.make_async_copy(src, dst, load_sem.at[i])
        for i, (src, dst) in enumerate(
            [(jumps_hbm, jumps), (base_hbm, base), (press_hbm, press), (tiles_hbm, tiles)]
        )
    ]
    for load in loads:
        load.start()

    barrier = pltpu.get_barrier_semaphore()
    for d in range(1, nr):
        peer = lax.rem(me_r + d, nr)
        pl.semaphore_signal(barrier, inc=1, device_id={"rock": peer}, device_id_type=MESH)
    for d in range(1, nf):
        peer = lax.rem(me_f + d, nf)
        pl.semaphore_signal(barrier, inc=1, device_id={"frac": peer}, device_id_type=MESH)
    for ident in (after_id, before_id):
        pl.semaphore_signal(barrier, inc=1, device_id=ident, device_id_type=MESH)

    loads[0].wait()

    def gap_step(k, _):
        rows = pl.ds(pl.multiple_of(k * LANES, LANES), LANES)
        a, b, c = jumps[0, rows, :], jumps[1, rows, :], jumps[2, rows, :]
        soft = jnp.maximum(a, 0.0) + jnp.log1p(jnp.exp(-jnp.abs(a)))
        gap[rows, :] = split_lanes(0.5 * soft + 0.2 * (jnp.sqrt(1.0 + b * b + c * c) - 1.0))
        return 0

    lax.fori_loop(0, eb // LANES, gap_step, 0)

    def face_rows(peer, m):
        row = face_ref[pl.ds(peer * nsub + m, 1), :]
        return fold(dot(one_hot(column(row), eb), gap[...]))

    def sub(m):
        return pl.ds(pl.multiple_of(m * LANES, LANES), LANES)

    def face_copy(peer, m, slot):
        return pltpu.make_async_remote_copy(
            src_ref=face_out.at[peer, sub(m)],
            dst_ref=face_in.at[slot, sub(m)],
            send_sem=face_ss.at[peer, m],
            recv_sem=face_rs.at[slot, m],
            device_id={"rock": peer},
            device_id_type=MESH,
        )

    pl.semaphore_wait(barrier, nr - 1 + nf - 1 + 2)

    def face_step(k, _):
        peer = lax.rem(me_r + 1 + k // nsub, nr)
        m = lax.rem(k, nsub)
        face_out[peer, sub(m), :] = face_rows(peer, m)
        face_copy(peer, m, me_r).start()
        return 0

    lax.fori_loop(0, (nr - 1) * nsub, face_step, 0)

    for g in range(2 * slots // LANES):
        pair_hot[g * LANES : (g + 1) * LANES, :] = one_hot(
            column(slot_ref[:, g * LANES : (g + 1) * LANES]), eb
        )
    loads[2].wait()

    def press_step(v, _):
        picked = fold(dot(pair_hot[...], split_lanes(press[v])))
        near_p[:, v] = picked[:slots].reshape(nf, cap, width)
        far_out[:, v] = picked[slots:].reshape(nf, cap, width)
        return 0

    lax.fori_loop(0, nv, press_step, 0)

    def far_copy(peer, slot):
        return pltpu.make_async_remote_copy(
            src_ref=far_out.at[peer],
            dst_ref=far_in.at[slot],
            send_sem=far_ss.at[peer],
            recv_sem=far_rs.at[slot],
            device_id={"frac": peer},
            device_id_type=MESH,
        )

    for d in range(1, nf):
        far_copy(lax.rem(me_f + d, nf), me_f).start()
    far_in[me_f] = far_out[me_f]

    def own_step(m, _):
        face_in[me_r, sub(m), :] = face_rows(me_r, m)
        return 0

    lax.fori_loop(0, nsub, own_step, 0)

    def elem_step(k, _):
        col = column(elem_ref[pl.ds(k, 1), :])
        for s in range(nr):
            elem_hot[s, sub(k), :] = one_hot(col - s * capf, capf)
        return 0

    lax.fori_loop(0, eb // LANES, elem_step, 0)

    loads[1].wait()
    acc[...] = base[...]

    def take(s):
        faces = split_lanes(face_in[s])

        def step(k, _):
            acc[sub(k), :] += fold(dot(elem_hot[s, sub(k), :], faces))
            return 0

        lax.fori_loop(0, eb // LANES, step, 0)

    take(me_r)
    for d in range(1, nr):
        source = lax.rem(me_r + nr - d, nr)
        for m in range(nsub):
            face_copy(source, m, source).wait_recv()
        take(source)

    aperture = acc[...]
    ap_ref[...] = aperture
    trans = aperture * aperture * aperture / 12.0

    picked_t = fold(dot(pair_hot[...], split_lanes(trans)))
    picked_t = jnp.where(picked_t == 0.0, 1.0, picked_t)
    near_t[...] = picked_t[:slots].reshape(nf, cap, width)
    trans_out[...] = picked_t[slots:].reshape(nf, cap, width)

    def trans_copy(peer, slot):
        return pltpu.make_async_remote_copy(
            src_ref=trans_out.at[peer],
            dst_ref=trans_in.at[slot],
            send_sem=trans_ss.at[peer],
            recv_sem=trans_rs.at[slot],
            device_id={"frac": peer},
            device_id_type=MESH,
        )

    for d in range(1, nf):
        trans_copy(lax.rem(me_f + d, nf), me_f).start()
    trans_in[me_f] = trans_out[me_f]

    for side, at in ((0, eb - 1), (1, 0)):
        for v in range(nv):
            edge_out[side, v : v + 1, :] = press[v, at : at + 1, :]
        edge_out[side, nv : nv + 1, :] = trans[at : at + 1, :]
        edge_out[side, nv + 1 : nv + 2, :] = jnp.broadcast_to(
            frac_ref[at // width : at // width + 1, at % width : at % width + 1], (1, width)
        ).astype(F32)
        edge_out[side, nv + 2 :, :] = jnp.zeros((edge_out.shape[1] - nv - 2, width), F32)

    edges = [
        pltpu.make_async_remote_copy(
            src_ref=edge_out.at[side],
            dst_ref=dst,
            send_sem=edge_ss.at[side],
            recv_sem=edge_rs.at[side],
            device_id=ident,
            device_id_type=MESH,
        )
        for side, dst, ident in ((0, left_ref, after_id), (1, right_ref, before_id))
    ]
    for edge in edges:
        edge.start()

    def ret_copy(peer, slot):
        return pltpu.make_async_remote_copy(
            src_ref=ret_out.at[peer],
            dst_ref=ret_in.at[slot],
            send_sem=ret_ss.at[peer],
            recv_sem=ret_rs.at[slot],
            device_id={"frac": peer},
            device_id_type=MESH,
        )

    loads[3].wait()
    ones = jnp.ones((nv, 2 * width), BF16)
    none = jnp.zeros((nv, width), BF16)

    def terms_of(q):
        near_tr = jnp.concatenate(
            [near_t[q], jnp.ones((LANES - cap, width), F32)], axis=0
        ).T
        far_tr = trans_in[q]
        for c in range(cap):
            n = near_tr[:, c : c + 1]
            f = far_tr[c : c + 1, :]
            w = tiles[q * cap + c].astype(F32) * (2.0 * n * f / (n + f))
            hi, lo = split(w)
            pn = near_p[q, :, c, :]
            pf = far_in[q, :, c, :]
            left = jnp.concatenate(
                [jnp.concatenate([pf.astype(BF16), none], axis=1), ones], axis=0
            )
            both = dot_nt(left, jnp.concatenate([hi, lo], axis=1))
            near_term[q, :, c, :] = both[nv:] * pn - both[:nv]
            ret_out[q, :, c, :] = jnp.sum(w, axis=0, keepdims=True) * pf - dot(
                pn.astype(BF16), hi
            )

    def terms_step(d, _):
        q = lax.rem(me_f + nf - d, nf)
        trans_copy(q, q).wait_recv()
        far_copy(q, q).wait_recv()
        terms_of(q)
        ret_copy(q, me_f).start()
        return 0

    lax.fori_loop(1, nf, terms_step, 0)
    terms_of(me_f)
    ret_in[me_f] = ret_out[me_f]

    for v in range(nv):
        hi, lo = split(near_term[:, v].reshape(slots, width))
        terms_ref[v, :slots, :] = hi
        terms_ref[v, 2 * slots : 3 * slots, :] = lo

    for d in range(1, nf):
        q = lax.rem(me_f + nf - d, nf)
        ret_copy(q, q).wait_recv()

    for v in range(nv):
        hi, lo = split(ret_in[:, v].reshape(slots, width))
        terms_ref[v, slots : 2 * slots, :] = hi
        terms_ref[v, 3 * slots :, :] = lo

    for edge in edges:
        edge.wait()
    for d in range(1, nr):
        peer = lax.rem(me_r + d, nr)
        for m in range(nsub):
            face_copy(peer, m, me_r).wait_send()
    for d in range(1, nf):
        peer = lax.rem(me_f + d, nf)
        far_copy(peer, me_f).wait_send()
        trans_copy(peer, me_f).wait_send()
        ret_copy(peer, me_f).wait_send()


def harmonic(a, b):
    return 2.0 * a * b / (a + b)


def image_kernel(
    count,
    p_ref,
    pl_ref,
    pr_ref,
    a_ref,
    al_ref,
    ar_ref,
    frac_ref,
    left_ref,
    right_ref,
    slot_ref,
    terms_ref,
    out_ref,
    ap_ref,
):
    nv, rows, width = p_ref.shape
    halo = pl_ref.shape[1]
    i = pl.program_id(0)
    n = pl.num_programs(0)
    first = i == 0
    last = i == n - 1
    me = lax.axis_index("rock") * lax.axis_size("frac") + lax.axis_index("frac")
    has_left = jnp.where(first & (me == 0), 0.0, 1.0)
    has_right = jnp.where(last & (me == count - 1), 0.0, 1.0)
    lane = lax.broadcasted_iota(jnp.int32, (rows, width), 1)
    row = lax.broadcasted_iota(jnp.int32, (rows, width), 0)
    first_lane, last_lane = lane == 0, lane == width - 1
    first_row, last_row = row == 0, row == rows - 1

    def up(x, nxt):
        below = jnp.where(last_row, nxt, pltpu.roll(x, rows - 1, 0))
        return pltpu.roll(jnp.where(first_lane, below, x), width - 1, 1)

    def down(x, prv):
        above = jnp.where(first_row, prv, pltpu.roll(x, 1, 0))
        return pltpu.roll(jnp.where(last_lane, above, x), 1, 1)

    a = a_ref[...]
    ap_ref[...] = a

    def tr(x):
        return x * x * x / 12.0

    t = tr(a)
    t_prv = jnp.where(first, left_ref[nv : nv + 1, :], tr(al_ref[halo - 1 :, :]))
    t_nxt = jnp.where(last, right_ref[nv : nv + 1, :], tr(ar_ref[:1, :]))

    fr_row = frac_ref[pl.ds(i, 1), :].astype(F32)
    fr = jnp.broadcast_to(fr_row, (rows, width)).T
    fr_left = frac_ref[pl.ds(jnp.maximum(i - 1, 0), 1), :].astype(F32)[:, width - 1 :]
    fr_right = frac_ref[pl.ds(jnp.minimum(i + 1, n - 1), 1), :].astype(F32)[:, :1]
    fr_prv = jnp.where(first, left_ref[nv + 1 : nv + 2, :1], fr_left)
    fr_nxt = jnp.where(last, right_ref[nv + 1 : nv + 2, :1], fr_right)
    fr_below = jnp.where(last_row, fr_nxt, pltpu.roll(fr, rows - 1, 0))
    joined = jnp.where(last_row & last_lane, has_right, 1.0) * jnp.where(
        last_lane & (fr_below != fr), 0.0, 1.0
    )
    h = harmonic(t, up(t, t_nxt)) * joined
    joined_prv = jnp.where(fr_prv == fr[:1, :], 1.0, 0.0) * has_left
    h_prv = harmonic(t_prv, pltpu.roll(t[:8], width - 1, 1)[:1]) * joined_prv

    ids = i * rows + lax.broadcasted_iota(jnp.int32, (rows, slot_ref.shape[1]), 0)
    hot = jnp.where(ids == slot_ref[...], 1.0, 0.0).astype(BF16)

    for v in range(nv):
        p = p_ref[v]
        p_prv = jnp.where(first, left_ref[v : v + 1, :], pl_ref[v, halo - 1 :, :])
        p_nxt = jnp.where(last, right_ref[v : v + 1, :], pr_ref[v, :1, :])
        flux = h * (p - up(p, p_nxt))
        flux_prv = h_prv * (p_prv - pltpu.roll(p[:8], width - 1, 1)[:1])
        out_ref[v] = a * p + flux - down(flux, flux_prv) + dot(hot, terms_ref[v])


def per_device(
    jumps,
    base_aperture,
    pressure,
    block_fracture,
    send_face,
    elem_source,
    pair_local,
    send_block,
    tiles,
):
    nr, nf = lax.axis_size("rock"), lax.axis_size("frac")
    nv, eb, width = pressure.shape
    slots = pair_local.shape[0]
    cap = slots // nf
    capf = send_face.shape[0] // nr
    nsub = capf // LANES
    edge_rows = -(-(nv + 2) // 8) * 8
    frac = block_fracture.reshape(eb // LANES, LANES)
    slot_row = jnp.concatenate([pair_local, send_block, pair_local, send_block]).reshape(1, -1)
    any_spec = pl.BlockSpec(memory_space=pl.ANY)
    vmem = pl.BlockSpec(memory_space=pltpu.VMEM)
    dma = pltpu.SemaphoreType.DMA
    peers = (nf, nv, cap, width)
    aperture, terms, left, right = pl.pallas_call(
        functools.partial(exchange_kernel, nr, nf),
        out_shape=(
            jax.ShapeDtypeStruct((eb, width), F32),
            jax.ShapeDtypeStruct((nv, 4 * slots, width), BF16),
            jax.ShapeDtypeStruct((edge_rows, width), F32),
            jax.ShapeDtypeStruct((edge_rows, width), F32),
        ),
        in_specs=[any_spec] * 4 + [vmem] * 4,
        out_specs=(vmem,) * 4,
        scratch_shapes=[
            pltpu.VMEM((3, eb, width), F32),
            pltpu.VMEM((eb, width), F32),
            pltpu.VMEM((nv, eb, width), F32),
            pltpu.VMEM((slots, width, width), BF16),
            pltpu.VMEM((eb, 2 * width), BF16),
            pltpu.VMEM((nr, capf, width), F32),
            pltpu.VMEM((nr, capf, width), F32),
            pltpu.VMEM((nr, eb, capf), BF16),
            pltpu.VMEM((2 * slots, eb), BF16),
            pltpu.VMEM((eb, width), F32),
            pltpu.VMEM(peers, F32),
            pltpu.VMEM(peers, F32),
            pltpu.VMEM(peers, F32),
            pltpu.VMEM((nf, cap, width), F32),
            pltpu.VMEM((nf, cap, width), F32),
            pltpu.VMEM((nf, cap, width), F32),
            pltpu.VMEM(peers, F32),
            pltpu.VMEM(peers, F32),
            pltpu.VMEM(peers, F32),
            pltpu.VMEM((2, edge_rows, width), F32),
            dma((4,)),
            dma((nr, nsub)),
            dma((nr, nsub)),
            dma((nf,)),
            dma((nf,)),
            dma((nf,)),
            dma((nf,)),
            dma((nf,)),
            dma((nf,)),
            dma((2,)),
            dma((2,)),
        ],
        compiler_params=pltpu.CompilerParams(
            collective_id=0, has_side_effects=True, vmem_limit_bytes=VMEM_LIMIT
        ),
        name="exchange",
    )(
        jumps,
        base_aperture,
        pressure,
        tiles,
        send_face.reshape(-1, LANES),
        elem_source.reshape(-1, LANES),
        slot_row,
        frac,
    )
    rows = LANES
    halo = 8
    step = rows // halo
    end = eb // halo - 1
    before = lambda i: jnp.maximum(i * step - 1, 0)
    after = lambda i: jnp.minimum((i + 1) * step, end)
    return pl.pallas_call(
        functools.partial(image_kernel, nr * nf),
        grid=(eb // rows,),
        out_shape=(
            jax.ShapeDtypeStruct((nv, eb, width), F32),
            jax.ShapeDtypeStruct((eb, width), F32),
        ),
        in_specs=[
            pl.BlockSpec((nv, rows, width), lambda i: (0, i, 0)),
            pl.BlockSpec((nv, halo, width), lambda i: (0, before(i), 0)),
            pl.BlockSpec((nv, halo, width), lambda i: (0, after(i), 0)),
            pl.BlockSpec((rows, width), lambda i: (i, 0)),
            pl.BlockSpec((halo, width), lambda i: (before(i), 0)),
            pl.BlockSpec((halo, width), lambda i: (after(i), 0)),
            vmem,
            vmem,
            vmem,
            vmem,
            vmem,
        ],
        out_specs=(
            pl.BlockSpec((nv, rows, width), lambda i: (0, i, 0)),
            pl.BlockSpec((rows, width), lambda i: (i, 0)),
        ),
        compiler_params=pltpu.CompilerParams(vmem_limit_bytes=VMEM_LIMIT),
        name="image",
    )(
        pressure,
        pressure,
        pressure,
        aperture,
        aperture,
        aperture,
        frac,
        left,
        right,
        slot_row,
        terms,
    )


def solution(mesh):
    split_axes = ("rock", "frac")
    return jax.shard_map(
        per_device,
        mesh=mesh,
        in_specs=(
            P(None, split_axes, None),
            P(split_axes, None),
            P(None, split_axes, None),
            P(split_axes),
            P(split_axes),
            P(split_axes),
            P(split_axes),
            P(split_axes),
            P(split_axes, None, None),
        ),
        out_specs=(P(None, split_axes, None), P(split_axes, None)),
        check_vma=False,
    )
```

```python
import functools

import jax
import jax.numpy as jnp
from jax import lax
from jax.experimental import pallas as pl
from jax.experimental.pallas import tpu as pltpu
from jax.sharding import PartitionSpec as P

MESH = pl.DeviceIdType.MESH
F32 = jnp.float32
BF16 = jnp.bfloat16
LANES = 128
VMEM_LIMIT = 60 * 1024 * 1024


def split(x):
    hi = x.astype(BF16)
    return hi, (x - hi.astype(F32)).astype(BF16)


def split_lanes(x):
    return jnp.concatenate(split(x), axis=1)


def fold(x):
    half = x.shape[1] // 2
    return x[:, :half] + x[:, half:]


def column(row):
    return jnp.broadcast_to(row, (LANES, LANES)).T


def one_hot(col, width):
    lane = lax.broadcasted_iota(jnp.int32, (LANES, LANES), 1)
    parts = [
        jnp.where(col == lane + k * LANES, 1.0, 0.0).astype(BF16) for k in range(width // LANES)
    ]
    return jnp.concatenate(parts, axis=1)


def dot(a, b):
    return jnp.dot(a, b, preferred_element_type=F32)


def dot_nt(a, b):
    return lax.dot_general(a, b, (((1,), (1,)), ((), ())), preferred_element_type=F32)


def exchange_kernel(
    nr,
    nf,
    jumps_hbm,
    base_hbm,
    press_hbm,
    tiles_hbm,
    face_ref,
    elem_ref,
    slot_ref,
    frac_ref,
    ap_ref,
    terms_ref,
    left_ref,
    right_ref,
    jumps,
    base,
    press,
    tiles,
    gap,
    face_out,
    face_in,
    elem_hot,
    pair_hot,
    acc,
    near_p,
    far_out,
    far_in,
    near_t,
    trans_out,
    trans_in,
    near_term,
    ret_out,
    ret_in,
    edge_out,
    load_sem,
    face_ss,
    face_rs,
    far_ss,
    far_rs,
    trans_ss,
    trans_rs,
    ret_ss,
    ret_rs,
    edge_ss,
    edge_rs,
):
    me_r = lax.axis_index("rock")
    me_f = lax.axis_index("frac")
    nv, eb, width = press.shape
    cap = far_in.shape[2]
    slots = nf * cap
    capf = face_in.shape[1]
    nsub = capf // LANES
    count = nr * nf
    me = me_r * nf + me_f
    after = lax.rem(me + 1, count)
    before = lax.rem(me + count - 1, count)
    after_id = (after // nf, lax.rem(after, nf))
    before_id = (before // nf, lax.rem(before, nf))

    loads = [
        pltpu.make_async_copy(src, dst, load_sem.at[i])
        for i, (src, dst) in enumerate(
            [(jumps_hbm, jumps), (base_hbm, base), (press_hbm, press), (tiles_hbm, tiles)]
        )
    ]
    for load in loads:
        load.start()

    barrier = pltpu.get_barrier_semaphore()
    for d in range(1, nr):
        peer = lax.rem(me_r + d, nr)
        pl.semaphore_signal(barrier, inc=1, device_id={"rock": peer}, device_id_type=MESH)
    for d in range(1, nf):
        peer = lax.rem(me_f + d, nf)
        pl.semaphore_signal(barrier, inc=1, device_id={"frac": peer}, device_id_type=MESH)
    for ident in (after_id, before_id):
        pl.semaphore_signal(barrier, inc=1, device_id=ident, device_id_type=MESH)

    loads[0].wait()

    def gap_step(k, _):
        rows = pl.ds(pl.multiple_of(k * LANES, LANES), LANES)
        a, b, c = jumps[0, rows, :], jumps[1, rows, :], jumps[2, rows, :]
        soft = jnp.maximum(a, 0.0) + jnp.log1p(jnp.exp(-jnp.abs(a)))
        gap[rows, :] = split_lanes(0.5 * soft + 0.2 * (jnp.sqrt(1.0 + b * b + c * c) - 1.0))
        return 0

    lax.fori_loop(0, eb // LANES, gap_step, 0, unroll=2)

    def face_rows(peer, m):
        row = face_ref[pl.ds(peer * nsub + m, 1), :]
        return fold(dot(one_hot(column(row), eb), gap[...]))

    def sub(m):
        return pl.ds(pl.multiple_of(m * LANES, LANES), LANES)

    def face_copy(peer, m, slot):
        return pltpu.make_async_remote_copy(
            src_ref=face_out.at[peer, sub(m)],
            dst_ref=face_in.at[slot, sub(m)],
            send_sem=face_ss.at[peer, m],
            recv_sem=face_rs.at[slot, m],
            device_id={"rock": peer},
            device_id_type=MESH,
        )

    pl.semaphore_wait(barrier, nr - 1 + nf - 1 + 2)

    def face_step(d, _):
        peer = lax.rem(me_r + d, nr)
        for m in range(nsub):
            face_out[peer, m * LANES : (m + 1) * LANES, :] = face_rows(peer, m)
        for m in range(nsub):
            face_copy(peer, m, me_r).start()
        return 0

    lax.fori_loop(1, nr, face_step, 0)

    for g in range(2 * slots // LANES):
        pair_hot[g * LANES : (g + 1) * LANES, :] = one_hot(
            column(slot_ref[:, g * LANES : (g + 1) * LANES]), eb
        )
    loads[2].wait()

    def press_step(v, _):
        picked = fold(dot(pair_hot[...], split_lanes(press[v])))
        near_p[:, v] = picked[:slots].reshape(nf, cap, width)
        far_out[:, v] = picked[slots:].reshape(nf, cap, width)
        return 0

    lax.fori_loop(0, nv, press_step, 0, unroll=4)

    def far_copy(peer, slot):
        return pltpu.make_async_remote_copy(
            src_ref=far_out.at[peer],
            dst_ref=far_in.at[slot],
            send_sem=far_ss.at[peer],
            recv_sem=far_rs.at[slot],
            device_id={"frac": peer},
            device_id_type=MESH,
        )

    for d in range(1, nf):
        far_copy(lax.rem(me_f + d, nf), me_f).start()
    far_in[me_f] = far_out[me_f]

    for m in range(nsub):
        face_in[me_r, m * LANES : (m + 1) * LANES, :] = face_rows(me_r, m)

    def elem_step(k, _):
        col = column(elem_ref[pl.ds(k, 1), :])
        for s in range(nr):
            elem_hot[s, sub(k), :] = one_hot(col - s * capf, capf)
        return 0

    lax.fori_loop(0, eb // LANES, elem_step, 0, unroll=2)

    loads[1].wait()
    acc[...] = base[...]

    def take(s):
        faces = split_lanes(face_in[s])

        def step(k, _):
            acc[sub(k), :] += fold(dot(elem_hot[s, sub(k), :], faces))
            return 0

        lax.fori_loop(0, eb // LANES, step, 0, unroll=4)

    take(me_r)
    for d in range(1, nr):
        source = lax.rem(me_r + nr - d, nr)
        for m in range(nsub):
            face_copy(source, m, source).wait_recv()
        take(source)

    aperture = acc[...]
    ap_ref[...] = aperture
    trans = aperture * aperture * aperture / 12.0

    picked_t = fold(dot(pair_hot[...], split_lanes(trans)))
    picked_t = jnp.where(picked_t == 0.0, 1.0, picked_t)
    near_t[...] = picked_t[:slots].reshape(nf, cap, width)
    trans_out[...] = picked_t[slots:].reshape(nf, cap, width)

    def trans_copy(peer, slot):
        return pltpu.make_async_remote_copy(
            src_ref=trans_out.at[peer],
            dst_ref=trans_in.at[slot],
            send_sem=trans_ss.at[peer],
            recv_sem=trans_rs.at[slot],
            device_id={"frac": peer},
            device_id_type=MESH,
        )

    for d in range(1, nf):
        trans_copy(lax.rem(me_f + d, nf), me_f).start()
    trans_in[me_f] = trans_out[me_f]

    for side, at in ((0, eb - 1), (1, 0)):
        for v in range(nv):
            edge_out[side, v : v + 1, :] = press[v, at : at + 1, :]
        edge_out[side, nv : nv + 1, :] = trans[at : at + 1, :]
        edge_out[side, nv + 1 : nv + 2, :] = jnp.broadcast_to(
            frac_ref[at // width : at // width + 1, at % width : at % width + 1], (1, width)
        ).astype(F32)
        edge_out[side, nv + 2 :, :] = jnp.zeros((edge_out.shape[1] - nv - 2, width), F32)

    edges = [
        pltpu.make_async_remote_copy(
            src_ref=edge_out.at[side],
            dst_ref=dst,
            send_sem=edge_ss.at[side],
            recv_sem=edge_rs.at[side],
            device_id=ident,
            device_id_type=MESH,
        )
        for side, dst, ident in ((0, left_ref, after_id), (1, right_ref, before_id))
    ]
    for edge in edges:
        edge.start()

    def ret_copy(peer, slot):
        return pltpu.make_async_remote_copy(
            src_ref=ret_out.at[peer],
            dst_ref=ret_in.at[slot],
            send_sem=ret_ss.at[peer],
            recv_sem=ret_rs.at[slot],
            device_id={"frac": peer},
            device_id_type=MESH,
        )

    loads[3].wait()
    ones = jnp.ones((nv, 2 * width), BF16)
    none = jnp.zeros((nv, width), BF16)

    def terms_of(q):
        near_tr = jnp.concatenate(
            [near_t[q], jnp.ones((LANES - cap, width), F32)], axis=0
        ).T
        far_tr = trans_in[q]
        for c in range(cap):
            n = near_tr[:, c : c + 1]
            f = far_tr[c : c + 1, :]
            w = tiles[q * cap + c].astype(F32) * (2.0 * n * f / (n + f))
            hi, lo = split(w)
            pn = near_p[q, :, c, :]
            pf = far_in[q, :, c, :]
            left = jnp.concatenate(
                [jnp.concatenate([pf.astype(BF16), none], axis=1), ones], axis=0
            )
            both = dot_nt(left, jnp.concatenate([hi, lo], axis=1))
            near_term[q, :, c, :] = both[nv:] * pn - both[:nv]
            ret_out[q, :, c, :] = jnp.sum(w, axis=0, keepdims=True) * pf - dot(
                pn.astype(BF16), hi
            )

    def terms_step(d, _):
        q = lax.rem(me_f + nf - d, nf)
        trans_copy(q, q).wait_recv()
        far_copy(q, q).wait_recv()
        terms_of(q)
        ret_copy(q, me_f).start()
        return 0

    lax.fori_loop(1, nf, terms_step, 0)
    terms_of(me_f)
    ret_in[me_f] = ret_out[me_f]

    for v in range(nv):
        hi, lo = split(near_term[:, v].reshape(slots, width))
        pair, lanes = v // 2, slice(v % 2 * width, (v % 2 + 1) * width)
        terms_ref[pair, :slots, lanes] = hi
        terms_ref[pair, 2 * slots : 3 * slots, lanes] = lo

    for d in range(1, nf):
        q = lax.rem(me_f + nf - d, nf)
        ret_copy(q, q).wait_recv()

    for v in range(nv):
        hi, lo = split(ret_in[:, v].reshape(slots, width))
        pair, lanes = v // 2, slice(v % 2 * width, (v % 2 + 1) * width)
        terms_ref[pair, slots : 2 * slots, lanes] = hi
        terms_ref[pair, 3 * slots :, lanes] = lo

    for edge in edges:
        edge.wait()
    for d in range(1, nr):
        peer = lax.rem(me_r + d, nr)
        for m in range(nsub):
            face_copy(peer, m, me_r).wait_send()
    for d in range(1, nf):
        peer = lax.rem(me_f + d, nf)
        far_copy(peer, me_f).wait_send()
        trans_copy(peer, me_f).wait_send()
        ret_copy(peer, me_f).wait_send()


def harmonic(a, b):
    return 2.0 * a * b / (a + b)


def image_kernel(
    count,
    p_ref,
    pl_ref,
    pr_ref,
    a_ref,
    al_ref,
    ar_ref,
    frac_ref,
    left_ref,
    right_ref,
    slot_ref,
    terms_ref,
    out_ref,
    ap_ref,
):
    nv, rows, width = p_ref.shape
    halo = pl_ref.shape[1]
    i = pl.program_id(0)
    n = pl.num_programs(0)
    first = i == 0
    last = i == n - 1
    me = lax.axis_index("rock") * lax.axis_size("frac") + lax.axis_index("frac")
    has_left = jnp.where(first & (me == 0), 0.0, 1.0)
    has_right = jnp.where(last & (me == count - 1), 0.0, 1.0)
    lane = lax.broadcasted_iota(jnp.int32, (rows, width), 1)
    row = lax.broadcasted_iota(jnp.int32, (rows, width), 0)
    first_lane, last_lane = lane == 0, lane == width - 1
    first_row, last_row = row == 0, row == rows - 1

    def up(x, nxt):
        below = jnp.where(last_row, nxt, pltpu.roll(x, rows - 1, 0))
        return pltpu.roll(jnp.where(first_lane, below, x), width - 1, 1)

    def down(x, prv):
        above = jnp.where(first_row, prv, pltpu.roll(x, 1, 0))
        return pltpu.roll(jnp.where(last_lane, above, x), 1, 1)

    a = a_ref[...]
    ap_ref[...] = a

    def tr(x):
        return x * x * x / 12.0

    t = tr(a)
    t_prv = jnp.where(first, left_ref[nv : nv + 1, :], tr(al_ref[halo - 1 :, :]))
    t_nxt = jnp.where(last, right_ref[nv : nv + 1, :], tr(ar_ref[:1, :]))

    fr_row = frac_ref[pl.ds(i, 1), :].astype(F32)
    fr = jnp.broadcast_to(fr_row, (rows, width)).T
    fr_left = frac_ref[pl.ds(jnp.maximum(i - 1, 0), 1), :].astype(F32)[:, width - 1 :]
    fr_right = frac_ref[pl.ds(jnp.minimum(i + 1, n - 1), 1), :].astype(F32)[:, :1]
    fr_prv = jnp.where(first, left_ref[nv + 1 : nv + 2, :1], fr_left)
    fr_nxt = jnp.where(last, right_ref[nv + 1 : nv + 2, :1], fr_right)
    fr_below = jnp.where(last_row, fr_nxt, pltpu.roll(fr, rows - 1, 0))
    joined = jnp.where(last_row & last_lane, has_right, 1.0) * jnp.where(
        last_lane & (fr_below != fr), 0.0, 1.0
    )
    h = harmonic(t, up(t, t_nxt)) * joined
    joined_prv = jnp.where(fr_prv == fr[:1, :], 1.0, 0.0) * has_left
    h_prv = harmonic(t_prv, pltpu.roll(t[:8], width - 1, 1)[:1]) * joined_prv

    h_dn = down(h, h_prv)
    centre = a + h + h_dn
    one = jnp.minimum(i, 0) + 1
    edge = lax.broadcasted_iota(jnp.int32, (8, width), 0)

    ids = i * rows + lax.broadcasted_iota(jnp.int32, (rows, slot_ref.shape[1]), 0)
    hot = jnp.where(ids == slot_ref[...], 1.0, 0.0).astype(BF16)

    for v in range(nv):
        if v % 2 == 0:
            cross = dot(hot, terms_ref[v // 2])
        p = p_ref[v]
        p_prv = jnp.where(first, left_ref[v : v + 1, :], pl_ref[v, halo - 1 :, :])
        p_nxt = jnp.where(last, right_ref[v : v + 1, :], pr_ref[v, :1, :])
        tail = jnp.where(edge == 7, p_nxt, pltpu.roll(p[rows - 8 :], 7, 0))
        head = jnp.where(edge == 0, p_prv, pltpu.roll(p[:8], 1, 0))
        below = jnp.concatenate([p_ref[v, pl.ds(one, rows - 8), :], tail], axis=0)
        above = jnp.concatenate([head, p_ref[v, pl.ds(one + 6, rows - 8), :]], axis=0)
        p_up = pltpu.roll(jnp.where(first_lane, below, p), width - 1, 1)
        p_dn = pltpu.roll(jnp.where(last_lane, above, p), 1, 1)
        out_ref[v] = centre * p - h * p_up - h_dn * p_dn + cross[:, v % 2 * width :][:, :width]


def per_device(
    jumps,
    base_aperture,
    pressure,
    block_fracture,
    send_face,
    elem_source,
    pair_local,
    send_block,
    tiles,
):
    nr, nf = lax.axis_size("rock"), lax.axis_size("frac")
    nv, eb, width = pressure.shape
    slots = pair_local.shape[0]
    cap = slots // nf
    capf = send_face.shape[0] // nr
    nsub = capf // LANES
    edge_rows = -(-(nv + 2) // 8) * 8
    frac = block_fracture.reshape(eb // LANES, LANES)
    slot_row = jnp.concatenate([pair_local, send_block, pair_local, send_block]).reshape(1, -1)
    any_spec = pl.BlockSpec(memory_space=pl.ANY)
    vmem = pl.BlockSpec(memory_space=pltpu.VMEM)
    dma = pltpu.SemaphoreType.DMA
    peers = (nf, nv, cap, width)
    aperture, terms, left, right = pl.pallas_call(
        functools.partial(exchange_kernel, nr, nf),
        out_shape=(
            jax.ShapeDtypeStruct((eb, width), F32),
            jax.ShapeDtypeStruct((nv // 2, 4 * slots, 2 * width), BF16),
            jax.ShapeDtypeStruct((edge_rows, width), F32),
            jax.ShapeDtypeStruct((edge_rows, width), F32),
        ),
        in_specs=[any_spec] * 4 + [vmem] * 4,
        out_specs=(vmem,) * 4,
        scratch_shapes=[
            pltpu.VMEM((3, eb, width), F32),
            pltpu.VMEM((eb, width), F32),
            pltpu.VMEM((nv, eb, width), F32),
            pltpu.VMEM((slots, width, width), BF16),
            pltpu.VMEM((eb, 2 * width), BF16),
            pltpu.VMEM((nr, capf, width), F32),
            pltpu.VMEM((nr, capf, width), F32),
            pltpu.VMEM((nr, eb, capf), BF16),
            pltpu.VMEM((2 * slots, eb), BF16),
            pltpu.VMEM((eb, width), F32),
            pltpu.VMEM(peers, F32),
            pltpu.VMEM(peers, F32),
            pltpu.VMEM(peers, F32),
            pltpu.VMEM((nf, cap, width), F32),
            pltpu.VMEM((nf, cap, width), F32),
            pltpu.VMEM((nf, cap, width), F32),
            pltpu.VMEM(peers, F32),
            pltpu.VMEM(peers, F32),
            pltpu.VMEM(peers, F32),
            pltpu.VMEM((2, edge_rows, width), F32),
            dma((4,)),
            dma((nr, nsub)),
            dma((nr, nsub)),
            dma((nf,)),
            dma((nf,)),
            dma((nf,)),
            dma((nf,)),
            dma((nf,)),
            dma((nf,)),
            dma((2,)),
            dma((2,)),
        ],
        compiler_params=pltpu.CompilerParams(
            collective_id=0, has_side_effects=True, vmem_limit_bytes=VMEM_LIMIT
        ),
        name="exchange",
    )(
        jumps,
        base_aperture,
        pressure,
        tiles,
        send_face.reshape(-1, LANES),
        elem_source.reshape(-1, LANES),
        slot_row,
        frac,
    )
    rows = LANES
    halo = 8
    step = rows // halo
    end = eb // halo - 1
    before = lambda i: jnp.maximum(i * step - 1, 0)
    after = lambda i: jnp.minimum((i + 1) * step, end)
    return pl.pallas_call(
        functools.partial(image_kernel, nr * nf),
        grid=(eb // rows,),
        out_shape=(
            jax.ShapeDtypeStruct((nv, eb, width), F32),
            jax.ShapeDtypeStruct((eb, width), F32),
        ),
        in_specs=[
            pl.BlockSpec((nv, rows, width), lambda i: (0, i, 0)),
            pl.BlockSpec((nv, halo, width), lambda i: (0, before(i), 0)),
            pl.BlockSpec((nv, halo, width), lambda i: (0, after(i), 0)),
            pl.BlockSpec((rows, width), lambda i: (i, 0)),
            pl.BlockSpec((halo, width), lambda i: (before(i), 0)),
            pl.BlockSpec((halo, width), lambda i: (after(i), 0)),
            vmem,
            vmem,
            vmem,
            vmem,
            vmem,
        ],
        out_specs=(
            pl.BlockSpec((nv, rows, width), lambda i: (0, i, 0)),
            pl.BlockSpec((rows, width), lambda i: (i, 0)),
        ),
        compiler_params=pltpu.CompilerParams(vmem_limit_bytes=VMEM_LIMIT),
        name="image",
    )(
        pressure,
        pressure,
        pressure,
        aperture,
        aperture,
        aperture,
        frac,
        left,
        right,
        slot_row,
        terms,
    )


def solution(mesh):
    split_axes = ("rock", "frac")
    return jax.shard_map(
        per_device,
        mesh=mesh,
        in_specs=(
            P(None, split_axes, None),
            P(split_axes, None),
            P(None, split_axes, None),
            P(split_axes),
            P(split_axes),
            P(split_axes),
            P(split_axes),
            P(split_axes),
            P(split_axes, None, None),
        ),
        out_specs=(P(None, split_axes, None), P(split_axes, None)),
        check_vma=False,
    )
```
